256 devices in a mesh: row: 16 (over y, x), col: 16 (over z, core).
Axes of the slice: x: 4, y: 4, z: 8, core: 2. Of those that a mesh axis runs over, the one named last changes fastest.
Arguments:
- features: bfloat16 [4096, 256, 512], P(('row', 'col')), may hold values from -6 to 6
- analysis: bfloat16 [4096, 64, 256], P(('row', 'col')), may hold values from -0.375 to 0.375
- transitions: bfloat16 [12, 4096, 64, 128], P(None, ('row', 'col')), may hold values from -0.5 to 0.5
- synthesis: bfloat16 [4096, 64, 256], P(('row', 'col')), may hold values from -0.75 to 0.75
Outputs:
- filtered: bfloat16 [4096, 256, 512], P(('row', 'col'))
The draws below stay inside these ranges and needn't reach their ends.
All inputs are finite; a program needn't handle non-finite values.
Results may differ from the reference program's by a relative error of at most 0.02.
Values may be sent and summed in bfloat16 or wider, within the bound.
No kernel may reach another device: no remote copies, remote signals or barrier semaphores. Data moves between devices by JAX's collectives and lax.ppermute only.
A program may use at most 64 MiB of HBM per device.

```python
import jax
import jax.numpy as jnp
from jax import lax

RANK = 64
PTS = 256
LEAF_DEV = 16
LANES = 512
LEAF_BITS = 4
COL_BITS = 4
ROW_BITS = 4
LEVELS = 12
LEAVES = 4096
N_ROW = 16
N_COL = 16


def steps_of(rng, shape, cuts, low, top_value):
    loudness = 1.0
    for axis_at, parts in cuts:
        draws = jax.random.uniform(jax.random.fold_in(jax.random.fold_in(rng, 6), axis_at), (parts,), jnp.float32, low / len(cuts), top_value / len(cuts))
        loudness = loudness * jnp.repeat(jnp.exp(draws), shape[axis_at] // parts).reshape((-1,) + (1,) * (len(shape) - 1 - axis_at))
    return loudness


def normal_values(stream_key, extent, deviation, bound, cuts=(), held_as=jnp.bfloat16):
    drawn = deviation * jax.random.normal(stream_key, extent, jnp.float32)
    if cuts:
        drawn = drawn * steps_of(stream_key, extent, cuts, -0.22, 0.18)
    return jnp.clip(drawn, -bound, bound).astype(held_as)


def setup_inputs(seed: int = 0) -> dict:
    arg_keys = jax.random.split(jax.random.key(seed), 5)
    features = normal_values(arg_keys[0], (LEAVES, PTS, LANES), 1.0, 6.0, ((0, 256),))
    analysis = normal_values(arg_keys[1], (LEAVES, RANK, PTS), PTS ** -0.5, 0.375, ((0, 256),))
    transitions = normal_values(arg_keys[2], (LEVELS, LEAVES, RANK, 2 * RANK), (2 * RANK) ** -0.5, 0.5, ((1, 256),))
    synthesis = normal_values(arg_keys[3], (LEAVES, RANK, PTS), RANK ** -0.5, 0.75, ((0, 256),))
    return {"features": features, "analysis": analysis, "transitions": transitions, "synthesis": synthesis}


def merge_level(blocks, weights, bit_pos):
    block_count = blocks.shape[0]
    rank_size = blocks.shape[1]
    lane_count = blocks.shape[2]
    stride = 2 ** bit_pos
    groups = block_count // (2 * stride)
    paired = blocks.reshape(groups, 2, stride, rank_size, lane_count)
    joined = jnp.concatenate([paired[:, 0], paired[:, 1]], axis=2).astype(jnp.float32)
    mixing = weights.reshape(groups, 2, stride, rank_size, 2 * rank_size).astype(jnp.float32)
    merged = jnp.einsum("hbsrk,hskc->hbsrc", mixing, joined)
    return merged.reshape(block_count, rank_size, lane_count).astype(jnp.bfloat16)


def analyse(pieces):
    return jnp.einsum("lrp,lpc->lrc", pieces[0].astype(jnp.float32), pieces[1].astype(jnp.float32)).astype(jnp.bfloat16)


def synthesise(pieces):
    return jnp.einsum("lrp,lrc->lpc", pieces[0].astype(jnp.float32), pieces[1].astype(jnp.float32)).astype(jnp.bfloat16)


def reference(features, analysis, transitions, synthesis):
    groups = LEAVES // LEAF_DEV
    blocks = lax.map(analyse, (analysis.reshape(groups, LEAF_DEV, RANK, PTS), features.reshape(groups, LEAF_DEV, PTS, LANES)))
    blocks = blocks.reshape(LEAVES, RANK, LANES)
    for level_index in range(LEAF_BITS + COL_BITS):
        blocks = merge_level(blocks, transitions[level_index], level_index)
    blocks = blocks.reshape(N_ROW, N_COL, N_ROW, LEAF_DEV // N_ROW, RANK, LANES)
    blocks = jnp.transpose(blocks, (2, 1, 0, 3, 4, 5)).reshape(LEAVES, RANK, LANES)
    for level_index in range(ROW_BITS):
        blocks = merge_level(blocks, transitions[LEAF_BITS + COL_BITS + level_index], LEAF_BITS - ROW_BITS + level_index)
    filtered = lax.map(synthesise, (synthesis.reshape(groups, LEAF_DEV, RANK, PTS), blocks.reshape(groups, LEAF_DEV, RANK, LANES)))
    return filtered.reshape(LEAVES, PTS, LANES)
```

```python
import functools

import jax
import jax.numpy as jnp
from jax import lax
from jax.experimental import pallas as pl
from jax.experimental.pallas import tpu as pltpu
from jax.sharding import PartitionSpec as P


RANK = 64
LANES = 512
PTS = 256
SLOTS = 16
N_ROW = 16
N_COL = 16
N_Z = 8
HOST_LEVELS = 3
MSG = LANES + HOST_LEVELS * 2 * RANK
BF = jnp.bfloat16
F32 = jnp.float32
VMEM = pl.BlockSpec(memory_space=pltpu.VMEM)


def spread(r):
    return r ^ ((r << 1) & 14)


def gather(v):
    return v ^ ((v << 1) & 14) ^ ((v << 2) & 12) ^ ((v << 3) & 8)


def z_swap(array, d):
    return lax.ppermute(array, "col", [(c, c ^ (2 * d)) for c in range(N_COL)])


def to_target_row(array, b):
    pairs = []
    for r in range(N_ROW):
        for c in range(N_COL):
            pairs.append((r * N_COL + c, (spread(r) ^ (2 * (c >> 1)) ^ b) * N_COL + c))
    return lax.ppermute(array, ("row", "col"), pairs)


def dot(a, b):
    return lax.dot_general(a, b, (((1,), (0,)), ((), ())), preferred_element_type=F32)


def front_kernel(leaves, f_ref, a_ref, t_ref, o_ref):
    step = pl.program_id(0)
    for l in range(leaves):
        o_ref[step * leaves + l] = dot(a_ref[l], f_ref[l]).astype(BF)

    @pl.when(step == pl.num_programs(0) - 1)
    def _():
        for level in range(4):
            stride = 1 << level
            for lo in range(SLOTS):
                if lo & stride:
                    continue
                hi = lo + stride
                merge_pair(o_ref, t_ref.at[level], lo, hi)


def merge_pair(c_ref, t_ref, lo, hi):
    joined = jnp.concatenate([c_ref[lo], c_ref[hi]], axis=0)
    weights = jnp.concatenate([t_ref[lo], t_ref[hi]], axis=0)
    merged = dot(weights, joined).astype(BF)
    c_ref[lo] = merged[:RANK]
    c_ref[hi] = merged[RANK:]


def front(features, analysis, transitions):
    leaves = 2
    return pl.pallas_call(
        functools.partial(front_kernel, leaves),
        grid=(SLOTS // leaves,),
        in_specs=[
            pl.BlockSpec((leaves, PTS, LANES), lambda i: (i, 0, 0)),
            pl.BlockSpec((leaves, RANK, PTS), lambda i: (i, 0, 0)),
            pl.BlockSpec((4, SLOTS, RANK, 2 * RANK), lambda i: (0, 0, 0, 0)),
        ],
        out_specs=pl.BlockSpec((SLOTS, RANK, LANES), lambda i: (0, 0, 0)),
        out_shape=jax.ShapeDtypeStruct((SLOTS, RANK, LANES), BF),
        cost_estimate=pl.CostEstimate(flops=800_000_000, bytes_accessed=7_000_000, transcendentals=0),
        compiler_params=pltpu.CompilerParams(vmem_limit_bytes=12 << 20),
        name="front",
    )(features, analysis, transitions)


def message_kernel(b, r_ref, own_ref, partner_ref, t_ref, *outs):
    r, z, core = r_ref[0], r_ref[1], r_ref[2]
    for d in range(N_Z):
        host = z ^ d
        s = spread(r) ^ (2 * host) ^ b
        out = outs[d]
        t4 = t_ref[0, s]
        t4 = jnp.where(core == 0, t4, jnp.concatenate([t4[:, RANK:], t4[:, :RANK]], axis=1))
        joined = jnp.concatenate([own_ref[s], partner_ref[s]], axis=0)
        out[:, :LANES] = dot(t4, joined).astype(BF)
        for e in range(HOST_LEVELS):
            t = t_ref[1 + e, s]
            flipped = jnp.concatenate([t[:, RANK:], t[:, :RANK]], axis=1)
            bit = (host >> e) & 1
            out[:, LANES + e * 2 * RANK : LANES + (e + 1) * 2 * RANK] = jnp.where(bit == 0, t, flipped)


def messages(b, where, own, partner, transitions):
    return pl.pallas_call(
        functools.partial(message_kernel, b),
        grid=(1,),
        in_specs=[
            pl.BlockSpec(memory_space=pltpu.SMEM),
            VMEM,
            VMEM,
            pl.BlockSpec((4, SLOTS, RANK, 2 * RANK), lambda i: (1, 0, 0, 0)),
        ],
        out_specs=[VMEM] * N_Z,
        out_shape=[jax.ShapeDtypeStruct((RANK, MSG), BF)] * N_Z,
        cost_estimate=pl.CostEstimate(flops=70_000_000, bytes_accessed=3_000_000, transcendentals=0),
        compiler_params=pltpu.CompilerParams(vmem_limit_bytes=12 << 20),
        name=f"messages{b}",
    )(where, own, partner, transitions)


def host_kernel(*refs):
    msgs, out = refs[:N_Z], refs[N_Z]
    for e in range(HOST_LEVELS):
        stride = 1 << e
        lanes = slice(LANES + e * 2 * RANK, LANES + (e + 1) * 2 * RANK)
        for lo in range(N_Z):
            if lo & stride:
                continue
            hi = lo + stride
            if e == 0:
                joined = jnp.concatenate([msgs[lo][:, :LANES], msgs[hi][:, :LANES]], axis=0)
            else:
                joined = jnp.concatenate([out[lo], out[hi]], axis=0)
            weights = jnp.concatenate([msgs[lo][:, lanes], msgs[hi][:, lanes]], axis=0)
            merged = dot(weights, joined).astype(BF)
            out[lo] = merged[:RANK]
            out[hi] = merged[RANK:]


def host_merge(b, msgs):
    return pl.pallas_call(
        host_kernel,
        in_specs=[VMEM] * N_Z,
        out_specs=VMEM,
        out_shape=jax.ShapeDtypeStruct((N_Z, RANK, LANES), BF),
        cost_estimate=pl.CostEstimate(flops=200_000_000, bytes_accessed=1_400_000, transcendentals=0),
        compiler_params=pltpu.CompilerParams(vmem_limit_bytes=6 << 20),
        name=f"host{b}",
    )(*msgs)


def tail_kernel(leaves, r_ref, *refs):
    msgs, (t_ref, s_ref, o_ref, c_ref) = refs[: 2 * N_Z], refs[2 * N_Z :]
    step = pl.program_id(0)

    @pl.when(step == 0)
    def _():
        base = gather(r_ref[0] ^ (2 * r_ref[1]))
        for b in range(2):
            for d in range(N_Z):
                c_ref[base ^ gather(2 * d ^ b)] = msgs[b * N_Z + d][...]
        for level in range(4):
            stride = 1 << level
            for lo in range(SLOTS):
                if lo & stride:
                    continue
                merge_pair(c_ref, t_ref.at[level], lo, lo + stride)

    for l in range(leaves):
        o_ref[l] = lax.dot_general(
            s_ref[l], c_ref[step * leaves + l], (((0,), (0,)), ((), ())), preferred_element_type=F32
        ).astype(BF)


def tail(where, msgs, transitions, synthesis):
    leaves = 2
    return pl.pallas_call(
        functools.partial(tail_kernel, leaves),
        grid=(SLOTS // leaves,),
        in_specs=[pl.BlockSpec(memory_space=pltpu.SMEM)]
        + [VMEM] * (2 * N_Z)
        + [
            pl.BlockSpec((4, SLOTS, RANK, 2 * RANK), lambda i: (2, 0, 0, 0)),
            pl.BlockSpec((leaves, RANK, PTS), lambda i: (i, 0, 0)),
        ],
        out_specs=pl.BlockSpec((leaves, PTS, LANES), lambda i: (i, 0, 0)),
        out_shape=jax.ShapeDtypeStruct((SLOTS, PTS, LANES), BF),
        scratch_shapes=[pltpu.VMEM((SLOTS, RANK, LANES), BF)],
        cost_estimate=pl.CostEstimate(flops=800_000_000, bytes_accessed=7_000_000, transcendentals=0),
        compiler_params=pltpu.CompilerParams(vmem_limit_bytes=14 << 20),
        name="tail",
    )(where, *msgs, transitions, synthesis)


def on_device(features, analysis, transitions, synthesis):
    col = lax.axis_index("col")
    where = jnp.stack([lax.axis_index("row"), col >> 1, col & 1]).astype(jnp.int32)
    blocks = front(features, analysis, transitions)
    partner = lax.ppermute(blocks, "col", [(c, c ^ 1) for c in range(N_COL)])
    groups = []
    for b in range(2):
        sent = messages(b, where, blocks, partner, transitions)
        groups.append([sent[0]] + [z_swap(sent[d], d) for d in range(1, N_Z)])
    arrived = []
    for b in range(2):
        merged = to_target_row(host_merge(b, groups[b]), b)
        arrived += [merged[0]] + [z_swap(merged[d], d) for d in range(1, N_Z)]
    return tail(where, arrived, transitions, synthesis)


def solution(mesh):
    in_specs = (
        P(("row", "col"), None, None),
        P(("row", "col"), None, None),
        P(None, ("row", "col"), None, None),
        P(("row", "col"), None, None),
    )
    out_specs = P(("row", "col"), None, None)
    return jax.shard_map(
        on_device, mesh=mesh, in_specs=in_specs, out_specs=out_specs, check_vma=False
    )
```

```python
import functools

import jax
import jax.numpy as jnp
from jax import lax
from jax.experimental import pallas as pl
from jax.experimental.pallas import tpu as pltpu
from jax.sharding import PartitionSpec as P


RANK = 64
LANES = 512
PTS = 256
SLOTS = 16
N_ROW = 16
N_COL = 16
N_Z = 8
HOST_LEVELS = 3
MSG = LANES + HOST_LEVELS * 2 * RANK
BF = jnp.bfloat16
F32 = jnp.float32
VMEM = pl.BlockSpec(memory_space=pltpu.VMEM)


def spread(r):
    return r ^ ((r << 1) & 14)


def gather(v):
    return v ^ ((v << 1) & 14) ^ ((v << 2) & 12) ^ ((v << 3) & 8)


def z_swap(array, d):
    return lax.ppermute(array, "col", [(c, c ^ (2 * d)) for c in range(N_COL)])


def to_target_row(array, b):
    pairs = []
    for r in range(N_ROW):
        for c in range(N_COL):
            pairs.append((r * N_COL + c, (spread(r) ^ (2 * (c >> 1)) ^ b) * N_COL + c))
    return lax.ppermute(array, ("row", "col"), pairs)


def dot(a, b):
    return lax.dot_general(a, b, (((1,), (0,)), ((), ())), preferred_element_type=F32)


def ordered(bit, first, second):
    low = jnp.where(bit == 0, first, second)
    high = jnp.where(bit == 0, second, first)
    return jnp.concatenate([low, high], axis=0)


def front_kernel(leaves, f_ref, a_ref, t_ref, o_ref):
    step = pl.program_id(0)
    for l in range(leaves):
        o_ref[step * leaves + l] = dot(a_ref[l], f_ref[l]).astype(BF)

    @pl.when(step == pl.num_programs(0) - 1)
    def _():
        for level in range(4):
            stride = 1 << level
            for lo in range(SLOTS):
                if lo & stride:
                    continue
                hi = lo + stride
                merge_pair(o_ref, t_ref.at[level], lo, hi)


def merge_pair(c_ref, t_ref, lo, hi):
    joined = jnp.concatenate([c_ref[lo], c_ref[hi]], axis=0)
    weights = jnp.concatenate([t_ref[lo], t_ref[hi]], axis=0)
    merged = dot(weights, joined).astype(BF)
    c_ref[lo] = merged[:RANK]
    c_ref[hi] = merged[RANK:]


def front(features, analysis, transitions):
    leaves = 2
    return pl.pallas_call(
        functools.partial(front_kernel, leaves),
        grid=(SLOTS // leaves,),
        in_specs=[
            pl.BlockSpec((leaves, PTS, LANES), lambda i: (i, 0, 0)),
            pl.BlockSpec((leaves, RANK, PTS), lambda i: (i, 0, 0)),
            pl.BlockSpec((4, SLOTS, RANK, 2 * RANK), lambda i: (0, 0, 0, 0)),
        ],
        out_specs=pl.BlockSpec((SLOTS, RANK, LANES), lambda i: (0, 0, 0)),
        out_shape=jax.ShapeDtypeStruct((SLOTS, RANK, LANES), BF),
        cost_estimate=pl.CostEstimate(flops=800_000_000, bytes_accessed=7_000_000, transcendentals=0),
        compiler_params=pltpu.CompilerParams(vmem_limit_bytes=60 << 20),
        name="front",
    )(features, analysis, transitions)


def message_kernel(b, r_ref, own_ref, partner_ref, t_ref, *outs):
    r, z, core = r_ref[0], r_ref[1], r_ref[2]
    for d in range(N_Z):
        host = z ^ d
        s = spread(r) ^ (2 * host) ^ b
        out = outs[d]
        own, partner = own_ref[s], partner_ref[s]
        joined = ordered(core, own, partner)
        out[:, :LANES] = dot(t_ref[0, s], joined).astype(BF)
        for e in range(HOST_LEVELS):
            out[:, LANES + e * 2 * RANK : LANES + (e + 1) * 2 * RANK] = t_ref[1 + e, s]


def messages(b, where, own, partner, transitions):
    return pl.pallas_call(
        functools.partial(message_kernel, b),
        grid=(1,),
        in_specs=[
            pl.BlockSpec(memory_space=pltpu.SMEM),
            VMEM,
            VMEM,
            pl.BlockSpec((4, SLOTS, RANK, 2 * RANK), lambda i: (1, 0, 0, 0)),
        ],
        out_specs=[VMEM] * N_Z,
        out_shape=[jax.ShapeDtypeStruct((RANK, MSG), BF)] * N_Z,
        cost_estimate=pl.CostEstimate(flops=70_000_000, bytes_accessed=3_000_000, transcendentals=0),
        compiler_params=pltpu.CompilerParams(vmem_limit_bytes=12 << 20),
    )(where, own, partner, transitions)


def host_kernel(r_ref, *refs):
    msgs, out = refs[:N_Z], refs[N_Z]
    for e in range(HOST_LEVELS):
        stride = 1 << e
        bit = (r_ref[1] >> e) & 1
        lanes = slice(LANES + e * 2 * RANK, LANES + (e + 1) * 2 * RANK)
        for lo in range(N_Z):
            if lo & stride:
                continue
            hi = lo + stride
            if e == 0:
                joined = ordered(bit, msgs[lo][:, :LANES], msgs[hi][:, :LANES])
            else:
                joined = ordered(bit, out[lo], out[hi])
            weights = jnp.concatenate([msgs[lo][:, lanes], msgs[hi][:, lanes]], axis=0)
            merged = dot(weights, joined).astype(BF)
            out[lo] = merged[:RANK]
            out[hi] = merged[RANK:]


def host_merge(where, msgs):
    return pl.pallas_call(
        host_kernel,
        in_specs=[pl.BlockSpec(memory_space=pltpu.SMEM)] + [VMEM] * N_Z,
        out_specs=VMEM,
        out_shape=jax.ShapeDtypeStruct((N_Z, RANK, LANES), BF),
        cost_estimate=pl.CostEstimate(flops=200_000_000, bytes_accessed=1_400_000, transcendentals=0),
        compiler_params=pltpu.CompilerParams(vmem_limit_bytes=6 << 20),
    )(where, *msgs)


def tail_kernel(leaves, r_ref, *refs):
    msgs, (t_ref, s_ref, o_ref, c_ref) = refs[: 2 * N_Z], refs[2 * N_Z :]
    step = pl.program_id(0)

    @pl.when(step == 0)
    def _():
        base = gather(r_ref[0] ^ (2 * r_ref[1]))
        for b in range(2):
            for d in range(N_Z):
                c_ref[base ^ gather(2 * d ^ b)] = msgs[b * N_Z + d][...]
        for level in range(4):
            stride = 1 << level
            for lo in range(SLOTS):
                if lo & stride:
                    continue
                merge_pair(c_ref, t_ref.at[level], lo, lo + stride)

    for l in range(leaves):
        o_ref[l] = lax.dot_general(
            s_ref[l], c_ref[step * leaves + l], (((0,), (0,)), ((), ())), preferred_element_type=F32
        ).astype(BF)


def tail(where, msgs, transitions, synthesis):
    leaves = 2
    return pl.pallas_call(
        functools.partial(tail_kernel, leaves),
        grid=(SLOTS // leaves,),
        in_specs=[pl.BlockSpec(memory_space=pltpu.SMEM)]
        + [VMEM] * (2 * N_Z)
        + [
            pl.BlockSpec((4, SLOTS, RANK, 2 * RANK), lambda i: (2, 0, 0, 0)),
            pl.BlockSpec((leaves, RANK, PTS), lambda i: (i, 0, 0)),
        ],
        out_specs=pl.BlockSpec((leaves, PTS, LANES), lambda i: (i, 0, 0)),
        out_shape=jax.ShapeDtypeStruct((SLOTS, PTS, LANES), BF),
        scratch_shapes=[pltpu.VMEM((SLOTS, RANK, LANES), BF)],
        cost_estimate=pl.CostEstimate(flops=800_000_000, bytes_accessed=7_000_000, transcendentals=0),
        compiler_params=pltpu.CompilerParams(vmem_limit_bytes=14 << 20),
        name="tail",
    )(where, *msgs, transitions, synthesis)


FAR_FIRST = (4, 5, 3, 7, 6, 2, 1)


def pipeline(features, analysis, transitions, synthesis):
    col = lax.axis_index("col")
    where = jnp.stack([lax.axis_index("row"), col >> 1, col & 1]).astype(jnp.int32)
    blocks = front(features, analysis, transitions)
    partner = lax.ppermute(blocks, "col", [(c, c ^ 1) for c in range(N_COL)])
    groups = []
    for b in range(2):
        sent = messages(b, where, blocks, partner, transitions)
        group = list(sent)
        for d in FAR_FIRST:
            group[d] = z_swap(sent[d], d)
        groups.append(group)
    arrived = []
    for b in range(2):
        merged = host_merge(where, groups[b])
        merged = to_target_row(merged, b)
        group = [merged[0]] * N_Z
        for d in FAR_FIRST:
            group[d] = z_swap(merged[d], d)
        arrived += group
    return tail(where, arrived, transitions, synthesis)


def solution(mesh):
    in_specs = (
        P(("row", "col"), None, None),
        P(("row", "col"), None, None),
        P(None, ("row", "col"), None, None),
        P(("row", "col"), None, None),
    )
    out_specs = P(("row", "col"), None, None)
    return jax.shard_map(
        pipeline, mesh=mesh, in_specs=in_specs, out_specs=out_specs, check_vma=False
    )
```

```python
import functools

import jax
import jax.numpy as jnp
from jax import lax
from jax.experimental import pallas as pl
from jax.experimental.pallas import tpu as pltpu
from jax.sharding import PartitionSpec as P


RANK = 64
LANES = 512
PTS = 256
SLOTS = 16
N_ROW = 16
N_COL = 16
N_Z = 8
Z_LEVELS = 3
PAIR = 2 * RANK
MSG = LANES + Z_LEVELS * PAIR
BF = jnp.bfloat16
F32 = jnp.float32
VMEM = pl.BlockSpec(memory_space=pltpu.VMEM)
SMEM = pl.BlockSpec(memory_space=pltpu.SMEM)
HBM = pl.BlockSpec(memory_space=pltpu.HBM)
FAR_FIRST = (4, 5, 3, 7, 6, 2, 1)
FAR = (4, 5)
NEAR = (3, 7, 6, 2, 1)


def base_of(r_ref):
    return r_ref[0] ^ r_ref[1] ^ (10 * r_ref[2])


def z_swap(array, d):
    return lax.ppermute(array, "col", [(c, c ^ (2 * d)) for c in range(N_COL)])


def to_target_row(array, b, d=0):
    pairs = []
    for r in range(N_ROW):
        for c in range(N_COL):
            to_col = c ^ (2 * d)
            to_row = r ^ (to_col >> 1) ^ (8 * b) ^ (10 * (c & 1))
            pairs.append((r * N_COL + c, to_row * N_COL + to_col))
    return lax.ppermute(array, ("row", "col"), pairs)


def dot(a, b):
    return lax.dot_general(a, b, (((1,), (0,)), ((), ())), preferred_element_type=F32)


def merge_pair(c_ref, lo, hi, t_lo, t_hi):
    joined = jnp.concatenate([c_ref[lo], c_ref[hi]], axis=0)
    merged = dot(jnp.concatenate([t_lo, t_hi], axis=0), joined).astype(BF)
    c_ref[lo] = merged[:RANK]
    c_ref[hi] = merged[RANK:]


def front_kernel(f_hbm, a_hbm, t_hbm, c_ref, f_buf, a_buf, t_buf, f_sem, t_sem, a_sem):
    f_copies = [pltpu.make_async_copy(f_hbm.at[l], f_buf.at[l], f_sem.at[l]) for l in range(SLOTS)]
    a_copies = [
        pltpu.make_async_copy(a_hbm.at[pl.ds(4 * i, 4)], a_buf.at[pl.ds(4 * i, 4)], a_sem.at[i]) for i in range(4)
    ]
    t_copies = [pltpu.make_async_copy(t_hbm.at[e], t_buf.at[e], t_sem.at[e]) for e in range(4)]
    for l in range(SLOTS):
        if l % 4 == 0:
            a_copies[l // 4].start()
        f_copies[l].start()
        if l in (3, 7):
            t_copies[2 * (l // 4)].start()
            t_copies[2 * (l // 4) + 1].start()

    def level(e, first, count):
        stride = 1 << e
        for lo in range(first, first + count):
            if not lo & stride:
                merge_pair(c_ref, lo, lo + stride, t_buf[e, lo], t_buf[e, lo + stride])

    for group in range(4):
        a_copies[group].wait()
        for l in range(4 * group, 4 * group + 4):
            f_copies[l].wait()
        if group == 1:
            t_copies[0].wait()
            t_copies[1].wait()
        if group == 3:
            t_copies[2].wait()
            t_copies[3].wait()
        for l in range(4 * group, 4 * group + 4):
            c_ref[l] = dot(a_buf[l], f_buf[l]).astype(BF)
        if group:
            level(0, 4 * group - 4, 4)
            level(1, 4 * group - 4, 4)
        if group == 3:
            level(2, 0, 8)
    level(0, 12, 4)
    level(1, 12, 4)
    level(2, 8, 8)
    level(3, 0, 16)


def front(features, analysis, transitions):
    return pl.pallas_call(
        front_kernel,
        in_specs=[HBM] * 3,
        out_specs=VMEM,
        out_shape=jax.ShapeDtypeStruct((SLOTS, RANK, LANES), BF),
        scratch_shapes=[
            pltpu.VMEM((SLOTS, PTS, LANES), BF),
            pltpu.VMEM((SLOTS, RANK, PTS), BF),
            pltpu.VMEM((4, SLOTS, RANK, PAIR), BF),
            pltpu.SemaphoreType.DMA((SLOTS,)),
            pltpu.SemaphoreType.DMA((4,)),
            pltpu.SemaphoreType.DMA((4,)),
        ],
        cost_estimate=pl.CostEstimate(flops=800_000_000, bytes_accessed=7_000_000, transcendentals=0),
        compiler_params=pltpu.CompilerParams(vmem_limit_bytes=65_600_000),
        name="front",
    )(features, analysis, transitions)


def message_kernel(b, r_ref, own_ref, partner_ref, t_ref, *outs):
    base = base_of(r_ref)
    for core in range(2):

        @pl.when(r_ref[2] == core)
        def _(low=partner_ref if core else own_ref, high=own_ref if core else partner_ref):
            for d in range(N_Z):
                s = base ^ (d | 8 * b)
                joined = jnp.concatenate([low[s], high[s]], axis=0)
                outs[d][:, :LANES] = dot(t_ref[0, s], joined).astype(BF)
                for e in range(Z_LEVELS):
                    outs[d][:, LANES + e * PAIR : LANES + (e + 1) * PAIR] = t_ref[1 + e, s]


def messages(b, where, own, partner, t_mid):
    return pl.pallas_call(
        functools.partial(message_kernel, b),
        in_specs=[SMEM, VMEM, VMEM, VMEM],
        out_specs=[VMEM] * N_Z,
        out_shape=[jax.ShapeDtypeStruct((RANK, MSG), BF)] * N_Z,
        cost_estimate=pl.CostEstimate(flops=70_000_000, bytes_accessed=3_000_000, transcendentals=0),
        compiler_params=pltpu.CompilerParams(vmem_limit_bytes=8 << 20),
    )(where, own, partner, t_mid)


def host_kernel(r_ref, *refs):
    msgs, (out, c_ref) = refs[:N_Z], refs[N_Z:]
    for d in range(N_Z):
        c_ref[r_ref[1] ^ d] = msgs[d][...]
    for e in range(Z_LEVELS):
        stride = 1 << e
        lanes = slice(LANES + e * PAIR, LANES + (e + 1) * PAIR)
        for lo in range(N_Z):
            if lo & stride:
                continue
            hi = lo + stride
            joined = jnp.concatenate([c_ref[lo, :, :LANES], c_ref[hi, :, :LANES]], axis=0)
            weights = jnp.concatenate([c_ref[lo, :, lanes], c_ref[hi, :, lanes]], axis=0)
            merged = dot(weights, joined).astype(BF)
            for z, block in ((lo, merged[:RANK]), (hi, merged[RANK:])):
                if e < Z_LEVELS - 1:
                    c_ref[z, :, :LANES] = block
                else:
                    out[r_ref[1] ^ z] = block


def host_merge(where, msgs):
    return pl.pallas_call(
        host_kernel,
        in_specs=[SMEM] + [VMEM] * N_Z,
        out_specs=VMEM,
        out_shape=jax.ShapeDtypeStruct((N_Z, RANK, LANES), BF),
        scratch_shapes=[pltpu.VMEM((N_Z, RANK, MSG), BF)],
        cost_estimate=pl.CostEstimate(flops=200_000_000, bytes_accessed=1_400_000, transcendentals=0),
        compiler_params=pltpu.CompilerParams(vmem_limit_bytes=6 << 20),
    )(where, *msgs)


def half_levels(b, r_ref, msgs, t_ref, c_ref):
    base = base_of(r_ref)
    top = (base & 8) ^ (8 * b)
    for d in range(N_Z):
        c_ref[base ^ (d | 8 * b)] = msgs[d][...]
    for e in range(3):
        stride = 1 << e
        for j in range(N_Z):
            if j & stride:
                continue
            lo, hi = top + j, top + j + stride
            merge_pair(c_ref, lo, hi, t_ref[e, lo], t_ref[e, hi])


def first_half_kernel(r_ref, *refs):
    msgs, (t_ref, c_ref) = refs[:N_Z], refs[N_Z:]
    half_levels(0, r_ref, msgs, t_ref, c_ref)


def first_half(where, msgs, t_tail):
    return pl.pallas_call(
        first_half_kernel,
        in_specs=[SMEM] + [VMEM] * (N_Z + 1),
        out_specs=VMEM,
        out_shape=jax.ShapeDtypeStruct((SLOTS, RANK, LANES), BF),
        cost_estimate=pl.CostEstimate(flops=200_000_000, bytes_accessed=1_400_000, transcendentals=0),
        compiler_params=pltpu.CompilerParams(vmem_limit_bytes=6 << 20),
        name="first_half",
    )(where, *msgs, t_tail)


def tail_kernel(r_ref, *refs):
    msgs, (half_ref, t_ref, s_ref, o_hbm, c_ref, o_buf, sem) = refs[:N_Z], refs[N_Z:]
    base = base_of(r_ref)
    half_levels(1, r_ref, msgs, t_ref, c_ref)
    for j in range(N_Z):
        c_ref[(base & 8) + j] = half_ref[(base & 8) + j]
    copies = []
    for j in range(N_Z):
        merge_pair(c_ref, j, j + 8, t_ref[3, j], t_ref[3, j + 8])
        for l in (j, j + 8):
            o_buf[l] = lax.dot_general(
                s_ref[l], c_ref[l], (((0,), (0,)), ((), ())), preferred_element_type=F32
            ).astype(BF)
            copies.append(pltpu.make_async_copy(o_buf.at[l], o_hbm.at[l], sem.at[l]))
            copies[-1].start()
    for copy in copies:
        copy.wait()


def tail(where, msgs, half, t_tail, synthesis):
    return pl.pallas_call(
        tail_kernel,
        in_specs=[SMEM] + [VMEM] * (N_Z + 3),
        out_specs=HBM,
        out_shape=jax.ShapeDtypeStruct((SLOTS, PTS, LANES), BF),
        scratch_shapes=[
            pltpu.VMEM((SLOTS, RANK, LANES), BF),
            pltpu.VMEM((SLOTS, PTS, LANES), BF),
            pltpu.SemaphoreType.DMA((SLOTS,)),
        ],
        cost_estimate=pl.CostEstimate(flops=800_000_000, bytes_accessed=7_000_000, transcendentals=0),
        compiler_params=pltpu.CompilerParams(vmem_limit_bytes=14 << 20),
        name="tail",
    )(where, *msgs, half, t_tail, synthesis)


def pipeline(features, analysis, transitions, synthesis):
    col = lax.axis_index("col")
    where = jnp.stack([lax.axis_index("row"), col >> 1, col & 1]).astype(jnp.int32)
    blocks = front(features, analysis, transitions)
    t_mid, t_tail = transitions[4:8], transitions[8:12]
    partner = lax.ppermute(blocks, "col", [(c, c ^ 1) for c in range(N_COL)])
    groups = []
    for b in range(2):
        group = list(messages(b, where, blocks, partner, t_mid))
        for d in FAR_FIRST + (0,):
            if b:
                group[d] = to_target_row(group[d], b, d)
            elif d:
                group[d] = z_swap(group[d], d)
        groups.append(group)
    merged, arrived = [], []
    for b in range(2):
        blocks = host_merge(where, groups[b])
        if b == 0:
            blocks = to_target_row(blocks, 0)
        group = [blocks[0]] * N_Z
        for d in NEAR:
            group[d] = z_swap(blocks[d], d)
        merged.append(blocks)
        arrived.append(group)
    for d in FAR:
        pair = z_swap(jnp.stack([merged[0][d], merged[1][d]]), d)
        arrived[0][d], arrived[1][d] = pair[0], pair[1]
    half = first_half(where, arrived[0], t_tail)
    return tail(where, arrived[1], half, t_tail, synthesis)


def solution(mesh):
    in_specs = (
        P(("row", "col"), None, None),
        P(("row", "col"), None, None),
        P(None, ("row", "col"), None, None),
        P(("row", "col"), None, None),
    )
    out_specs = P(("row", "col"), None, None)
    return jax.shard_map(pipeline, mesh=mesh, in_specs=in_specs, out_specs=out_specs, check_vma=False)
```

```python
import functools

import jax
import jax.numpy as jnp
from jax import lax
from jax.experimental import pallas as pl
from jax.experimental.pallas import tpu as pltpu
from jax.sharding import PartitionSpec as P


RANK = 64
LANES = 512
PTS = 256
SLOTS = 16
N_ROW = 16
N_COL = 16
N_Z = 8
Z_LEVELS = 3
PAIR = 2 * RANK
MSG = LANES + Z_LEVELS * PAIR
BF = jnp.bfloat16
F32 = jnp.float32
VMEM = pl.BlockSpec(memory_space=pltpu.VMEM)
SMEM = pl.BlockSpec(memory_space=pltpu.SMEM)
HBM = pl.BlockSpec(memory_space=pltpu.HBM)
TOP = (8, 0)
TWIST = 6
FAR_FIRST = (4, 5, 3, 7, 6, 2, 1)
FAR = (4, 5, 3, 7, 6, 2, 1)
NEAR = ()


def base_of(r_ref):
    return r_ref[0] ^ r_ref[1] ^ (TWIST * r_ref[2])


def z_swap(array, d):
    return lax.ppermute(array, "col", [(c, c ^ (2 * d)) for c in range(N_COL)])


def to_target_row(array, b, d=0):
    pairs = []
    for r in range(N_ROW):
        for c in range(N_COL):
            to_col = c ^ (2 * d)
            to_row = r ^ (to_col >> 1) ^ TOP[b] ^ (TWIST * (c & 1))
            pairs.append((r * N_COL + c, to_row * N_COL + to_col))
    return lax.ppermute(array, ("row", "col"), pairs)


def dot(a, b):
    return lax.dot_general(a, b, (((1,), (0,)), ((), ())), preferred_element_type=F32)


def merge_pair(c_ref, lo, hi, t_lo, t_hi):
    joined = jnp.concatenate([c_ref[lo], c_ref[hi]], axis=0)
    merged = dot(jnp.concatenate([t_lo, t_hi], axis=0), joined).astype(BF)
    c_ref[lo] = merged[:RANK]
    c_ref[hi] = merged[RANK:]


def front_kernel(f_hbm, a_hbm, t_hbm, c_ref, f_buf, a_buf, t_buf, f_sem, t_sem, a_sem):
    f_copies = [pltpu.make_async_copy(f_hbm.at[l], f_buf.at[l], f_sem.at[l]) for l in range(SLOTS)]
    a_copies = [
        pltpu.make_async_copy(a_hbm.at[pl.ds(4 * i, 4)], a_buf.at[pl.ds(4 * i, 4)], a_sem.at[i]) for i in range(4)
    ]
    t_copies = [pltpu.make_async_copy(t_hbm.at[e], t_buf.at[e], t_sem.at[e]) for e in range(4)]
    for l in range(SLOTS):
        if l % 4 == 0:
            a_copies[l // 4].start()
        f_copies[l].start()
        if l in (3, 7):
            t_copies[2 * (l // 4)].start()
            t_copies[2 * (l // 4) + 1].start()

    def level(e, first, count):
        stride = 1 << e
        for lo in range(first, first + count):
            if not lo & stride:
                merge_pair(c_ref, lo, lo + stride, t_buf[e, lo], t_buf[e, lo + stride])

    for group in range(4):
        a_copies[group].wait()
        for l in range(4 * group, 4 * group + 4):
            f_copies[l].wait()
        if group == 1:
            t_copies[0].wait()
            t_copies[1].wait()
        if group == 3:
            t_copies[2].wait()
            t_copies[3].wait()
        for l in range(4 * group, 4 * group + 4):
            c_ref[l] = dot(a_buf[l], f_buf[l]).astype(BF)
        if group:
            level(0, 4 * group - 4, 4)
            level(1, 4 * group - 4, 4)
        if group == 3:
            level(2, 0, 8)
    level(0, 12, 4)
    level(1, 12, 4)
    level(2, 8, 8)
    level(3, 0, 16)


def front(features, analysis, transitions):
    return pl.pallas_call(
        front_kernel,
        in_specs=[HBM] * 3,
        out_specs=VMEM,
        out_shape=jax.ShapeDtypeStruct((SLOTS, RANK, LANES), BF),
        scratch_shapes=[
            pltpu.VMEM((SLOTS, PTS, LANES), BF),
            pltpu.VMEM((SLOTS, RANK, PTS), BF),
            pltpu.VMEM((4, SLOTS, RANK, PAIR), BF),
            pltpu.SemaphoreType.DMA((SLOTS,)),
            pltpu.SemaphoreType.DMA((4,)),
            pltpu.SemaphoreType.DMA((4,)),
        ],
        cost_estimate=pl.CostEstimate(flops=800_000_000, bytes_accessed=7_000_000, transcendentals=0),
        compiler_params=pltpu.CompilerParams(vmem_limit_bytes=65_600_000),
        name="front",
    )(features, analysis, transitions)


def message_kernel(b, r_ref, own_ref, partner_ref, t_ref, *outs):
    base, z = base_of(r_ref), r_ref[1]
    for core in range(2):

        @pl.when(r_ref[2] == core)
        def _(low=partner_ref if core else own_ref, high=own_ref if core else partner_ref):
            for d in range(N_Z):
                s = base ^ (d | TOP[b])
                joined = jnp.concatenate([low[s], high[s]], axis=0)
                outs[d][:, :LANES] = dot(t_ref[0, s], joined).astype(BF)
                for e in range(Z_LEVELS):
                    t = t_ref[1 + e, s]
                    flipped = jnp.concatenate([t[:, RANK:], t[:, :RANK]], axis=1)
                    host_bit = ((z ^ d) >> e) & 1
                    outs[d][:, LANES + e * PAIR : LANES + (e + 1) * PAIR] = jnp.where(host_bit == 0, t, flipped)


def messages(b, where, own, partner, t_mid):
    return pl.pallas_call(
        functools.partial(message_kernel, b),
        in_specs=[SMEM, VMEM, VMEM, VMEM],
        out_specs=[VMEM] * N_Z,
        out_shape=[jax.ShapeDtypeStruct((RANK, MSG), BF)] * N_Z,
        cost_estimate=pl.CostEstimate(flops=70_000_000, bytes_accessed=3_000_000, transcendentals=0),
        compiler_params=pltpu.CompilerParams(vmem_limit_bytes=8 << 20),
    )(where, own, partner, t_mid)


def host_kernel(*refs):
    msgs, out = refs[:N_Z], refs[N_Z]
    for e in range(Z_LEVELS):
        stride = 1 << e
        lanes = slice(LANES + e * PAIR, LANES + (e + 1) * PAIR)
        for lo in range(N_Z):
            if lo & stride:
                continue
            hi = lo + stride
            joined = [out[d] if e else msgs[d][:, :LANES] for d in (lo, hi)]
            weights = [msgs[d][:, lanes] for d in (lo, hi)]
            merged = dot(jnp.concatenate(weights, axis=0), jnp.concatenate(joined, axis=0)).astype(BF)
            out[lo] = merged[:RANK]
            out[hi] = merged[RANK:]


def host_merge(msgs):
    return pl.pallas_call(
        host_kernel,
        in_specs=[VMEM] * N_Z,
        out_specs=VMEM,
        out_shape=jax.ShapeDtypeStruct((N_Z, RANK, LANES), BF),
        cost_estimate=pl.CostEstimate(flops=200_000_000, bytes_accessed=1_400_000, transcendentals=0),
        compiler_params=pltpu.CompilerParams(vmem_limit_bytes=6 << 20),
    )(*msgs)


def half_levels(b, r_ref, msgs, t_ref, c_ref):
    base = base_of(r_ref)
    top = (base & 8) ^ TOP[b]
    for d in range(N_Z):
        c_ref[base ^ (d | TOP[b])] = msgs[d][...]
    for e in range(3):
        stride = 1 << e
        for j in range(N_Z):
            if j & stride:
                continue
            lo, hi = top + j, top + j + stride
            merge_pair(c_ref, lo, hi, t_ref[e, lo], t_ref[e, hi])


def first_half_kernel(r_ref, *refs):
    msgs, (t_ref, c_ref) = refs[:N_Z], refs[N_Z:]
    half_levels(0, r_ref, msgs, t_ref, c_ref)


def first_half(where, msgs, t_tail):
    return pl.pallas_call(
        first_half_kernel,
        in_specs=[SMEM] + [VMEM] * (N_Z + 1),
        out_specs=VMEM,
        out_shape=jax.ShapeDtypeStruct((SLOTS, RANK, LANES), BF),
        cost_estimate=pl.CostEstimate(flops=200_000_000, bytes_accessed=1_400_000, transcendentals=0),
        compiler_params=pltpu.CompilerParams(vmem_limit_bytes=6 << 20),
        name="first_half",
    )(where, *msgs, t_tail)


def tail_kernel(r_ref, *refs):
    msgs, (half_ref, t_ref, s_ref, o_hbm, c_ref, o_buf, sem) = refs[:N_Z], refs[N_Z:]
    base = base_of(r_ref)
    half_levels(1, r_ref, msgs, t_ref, c_ref)
    first = (base & 8) ^ TOP[0]
    for j in range(N_Z):
        c_ref[first + j] = half_ref[first + j]
    copies = []
    for j in range(N_Z):
        merge_pair(c_ref, j, j + 8, t_ref[3, j], t_ref[3, j + 8])
        for l in (j, j + 8):
            o_buf[l] = lax.dot_general(
                s_ref[l], c_ref[l], (((0,), (0,)), ((), ())), preferred_element_type=F32
            ).astype(BF)
            copies.append(pltpu.make_async_copy(o_buf.at[l], o_hbm.at[l], sem.at[l]))
            copies[-1].start()
    for copy in copies:
        copy.wait()


def tail(where, msgs, half, t_tail, synthesis):
    return pl.pallas_call(
        tail_kernel,
        in_specs=[SMEM] + [VMEM] * (N_Z + 3),
        out_specs=HBM,
        out_shape=jax.ShapeDtypeStruct((SLOTS, PTS, LANES), BF),
        scratch_shapes=[
            pltpu.VMEM((SLOTS, RANK, LANES), BF),
            pltpu.VMEM((SLOTS, PTS, LANES), BF),
            pltpu.SemaphoreType.DMA((SLOTS,)),
        ],
        cost_estimate=pl.CostEstimate(flops=800_000_000, bytes_accessed=7_000_000, transcendentals=0),
        compiler_params=pltpu.CompilerParams(vmem_limit_bytes=14 << 20),
        name="tail",
    )(where, *msgs, half, t_tail, synthesis)


def pipeline(features, analysis, transitions, synthesis):
    col = lax.axis_index("col")
    where = jnp.stack([lax.axis_index("row"), col >> 1, col & 1]).astype(jnp.int32)
    blocks = front(features, analysis, transitions)
    t_mid, t_tail = transitions[4:8], transitions[8:12]
    partner = lax.ppermute(blocks, "col", [(c, c ^ 1) for c in range(N_COL)])
    groups = []
    for b in range(2):
        group = list(messages(b, where, blocks, partner, t_mid))
        for d in FAR_FIRST + (0,):
            if b:
                group[d] = to_target_row(group[d], b, d)
            elif d:
                group[d] = z_swap(group[d], d)
        groups.append(group)
    merged, arrived = [], []
    for b in range(2):
        blocks = host_merge(groups[b])
        if b == 0:
            blocks = to_target_row(blocks, 0)
        group = [blocks[0]] * N_Z
        for d in NEAR:
            group[d] = z_swap(blocks[d], d)
        merged.append(blocks)
        arrived.append(group)
    for d in FAR:
        pair = z_swap(jnp.stack([merged[0][d], merged[1][d]]), d)
        arrived[0][d], arrived[1][d] = pair[0], pair[1]
    half = first_half(where, arrived[0], t_tail)
    return tail(where, arrived[1], half, t_tail, synthesis)


def solution(mesh):
    in_specs = (
        P(("row", "col"), None, None),
        P(("row", "col"), None, None),
        P(None, ("row", "col"), None, None),
        P(("row", "col"), None, None),
    )
    out_specs = P(("row", "col"), None, None)
    return jax.shard_map(pipeline, mesh=mesh, in_specs=in_specs, out_specs=out_specs, check_vma=False)
```

```python
import functools

import jax
import jax.numpy as jnp
from jax import lax
from jax.experimental import pallas as pl
from jax.experimental.pallas import tpu as pltpu
from jax.sharding import PartitionSpec as P


RANK = 64
LANES = 512
PTS = 256
SLOTS = 16
N_ROW = 16
N_COL = 16
N_Z = 8
Z_LEVELS = 3
PAIR = 2 * RANK
MSG = LANES + Z_LEVELS * PAIR
BF = jnp.bfloat16
F32 = jnp.float32
VMEM = pl.BlockSpec(memory_space=pltpu.VMEM)
SMEM = pl.BlockSpec(memory_space=pltpu.SMEM)
HBM = pl.BlockSpec(memory_space=pltpu.HBM)
TOP = (8, 0)
TWIST = 6
FAR_FIRST = (4, 5, 3, 7, 6, 2, 1)


def base_of(r_ref):
    return r_ref[0] ^ r_ref[1] ^ (TWIST * r_ref[2])


def z_swap(array, d):
    return lax.ppermute(array, "col", [(c, c ^ (2 * d)) for c in range(N_COL)])


def to_target_row(array, b, d=0):
    pairs = []
    for r in range(N_ROW):
        for c in range(N_COL):
            to_col = c ^ (2 * d)
            to_row = r ^ (to_col >> 1) ^ TOP[b] ^ (TWIST * (c & 1))
            pairs.append((r * N_COL + c, to_row * N_COL + to_col))
    return lax.ppermute(array, ("row", "col"), pairs)


def dot(a, b):
    return lax.dot_general(a, b, (((1,), (0,)), ((), ())), preferred_element_type=F32)


def merge_pair(c_ref, lo, hi, t_lo, t_hi):
    joined = jnp.concatenate([c_ref[lo], c_ref[hi]], axis=0)
    merged = dot(jnp.concatenate([t_lo, t_hi], axis=0), joined).astype(BF)
    c_ref[lo] = merged[:RANK]
    c_ref[hi] = merged[RANK:]


def front_kernel(f_hbm, a_hbm, t_hbm, c_ref, f_buf, a_buf, t_buf, f_sem, t_sem, a_sem):
    f_copies = [pltpu.make_async_copy(f_hbm.at[l], f_buf.at[l], f_sem.at[l]) for l in range(SLOTS)]
    a_copies = [
        pltpu.make_async_copy(a_hbm.at[pl.ds(4 * i, 4)], a_buf.at[pl.ds(4 * i, 4)], a_sem.at[i]) for i in range(4)
    ]
    t_copies = [pltpu.make_async_copy(t_hbm.at[e], t_buf.at[e], t_sem.at[e]) for e in range(4)]
    for l in range(SLOTS):
        if l % 4 == 0:
            a_copies[l // 4].start()
        f_copies[l].start()
        if l in (3, 7):
            t_copies[2 * (l // 4)].start()
            t_copies[2 * (l // 4) + 1].start()

    def level(e, first, count):
        stride = 1 << e
        for lo in range(first, first + count):
            if not lo & stride:
                merge_pair(c_ref, lo, lo + stride, t_buf[e, lo], t_buf[e, lo + stride])

    for group in range(4):
        a_copies[group].wait()
        for l in range(4 * group, 4 * group + 4):
            f_copies[l].wait()
        if group == 1:
            t_copies[0].wait()
            t_copies[1].wait()
        if group == 3:
            t_copies[2].wait()
            t_copies[3].wait()
        for l in range(4 * group, 4 * group + 4):
            c_ref[l] = dot(a_buf[l], f_buf[l]).astype(BF)
        if group:
            level(0, 4 * group - 4, 4)
            level(1, 4 * group - 4, 4)
        if group == 3:
            level(2, 0, 8)
    level(0, 12, 4)
    level(1, 12, 4)
    level(2, 8, 8)
    level(3, 0, 16)


def front(features, analysis, transitions):
    return pl.pallas_call(
        front_kernel,
        in_specs=[HBM] * 3,
        out_specs=VMEM,
        out_shape=jax.ShapeDtypeStruct((SLOTS, RANK, LANES), BF),
        scratch_shapes=[
            pltpu.VMEM((SLOTS, PTS, LANES), BF),
            pltpu.VMEM((SLOTS, RANK, PTS), BF),
            pltpu.VMEM((4, SLOTS, RANK, PAIR), BF),
            pltpu.SemaphoreType.DMA((SLOTS,)),
            pltpu.SemaphoreType.DMA((4,)),
            pltpu.SemaphoreType.DMA((4,)),
        ],
        cost_estimate=pl.CostEstimate(flops=800_000_000, bytes_accessed=7_000_000, transcendentals=0),
        compiler_params=pltpu.CompilerParams(vmem_limit_bytes=65_600_000),
        name="front",
    )(features, analysis, transitions)


def message_kernel(b, r_ref, own_ref, partner_ref, t_ref, *outs):
    base, z = base_of(r_ref), r_ref[1]
    for core in range(2):

        @pl.when(r_ref[2] == core)
        def _(low=partner_ref if core else own_ref, high=own_ref if core else partner_ref):
            for d in range(N_Z):
                s = base ^ (d | TOP[b])
                joined = jnp.concatenate([low[s], high[s]], axis=0)
                outs[d][:, :LANES] = dot(t_ref[0, s], joined).astype(BF)
                for e in range(Z_LEVELS):
                    t = t_ref[1 + e, s]
                    flipped = jnp.concatenate([t[:, RANK:], t[:, :RANK]], axis=1)
                    host_bit = ((z ^ d) >> e) & 1
                    outs[d][:, LANES + e * PAIR : LANES + (e + 1) * PAIR] = jnp.where(host_bit == 0, t, flipped)


def messages(b, where, own, partner, t_mid):
    return pl.pallas_call(
        functools.partial(message_kernel, b),
        in_specs=[SMEM, VMEM, VMEM, VMEM],
        out_specs=[VMEM] * N_Z,
        out_shape=[jax.ShapeDtypeStruct((RANK, MSG), BF)] * N_Z,
        cost_estimate=pl.CostEstimate(flops=70_000_000, bytes_accessed=3_000_000, transcendentals=0),
        compiler_params=pltpu.CompilerParams(vmem_limit_bytes=8 << 20),
    )(where, own, partner, t_mid)


def host_kernel(*refs):
    msgs, out = refs[:N_Z], refs[N_Z]
    for e in range(Z_LEVELS):
        stride = 1 << e
        lanes = slice(LANES + e * PAIR, LANES + (e + 1) * PAIR)
        for lo in range(N_Z):
            if lo & stride:
                continue
            hi = lo + stride
            joined = [out[d] if e else msgs[d][:, :LANES] for d in (lo, hi)]
            weights = [msgs[d][:, lanes] for d in (lo, hi)]
            merged = dot(jnp.concatenate(weights, axis=0), jnp.concatenate(joined, axis=0)).astype(BF)
            out[lo] = merged[:RANK]
            out[hi] = merged[RANK:]


def host_merge(msgs):
    return pl.pallas_call(
        host_kernel,
        in_specs=[VMEM] * N_Z,
        out_specs=VMEM,
        out_shape=jax.ShapeDtypeStruct((N_Z, RANK, LANES), BF),
        cost_estimate=pl.CostEstimate(flops=200_000_000, bytes_accessed=1_400_000, transcendentals=0),
        compiler_params=pltpu.CompilerParams(vmem_limit_bytes=6 << 20),
    )(*msgs)


def tail_kernel(r_ref, *refs):
    local, msgs, (t_ref, s_ref, o_hbm, c_ref, o_buf, sem) = refs[:2], refs[2 : 1 + N_Z], refs[1 + N_Z :]
    base = base_of(r_ref)
    for b in range(2):
        c_ref[base ^ TOP[b]] = local[b][0]
        for d in range(1, N_Z):
            c_ref[base ^ (d | TOP[b])] = msgs[d - 1][b]
    for e in range(3):
        for lo in range(SLOTS):
            if not (lo >> e) & 1:
                hi = lo + (1 << e)
                merge_pair(c_ref, lo, hi, t_ref[e, lo], t_ref[e, hi])
    copies = []
    for j in range(N_Z):
        merge_pair(c_ref, j, j + 8, t_ref[3, j], t_ref[3, j + 8])
        for l in (j, j + 8):
            o_buf[l] = lax.dot_general(
                s_ref[l], c_ref[l], (((0,), (0,)), ((), ())), preferred_element_type=F32
            ).astype(BF)
            copies.append(pltpu.make_async_copy(o_buf.at[l], o_hbm.at[l], sem.at[l]))
            copies[-1].start()
    for copy in copies:
        copy.wait()


def tail(where, local, msgs, t_tail, synthesis):
    return pl.pallas_call(
        tail_kernel,
        in_specs=[SMEM] + [VMEM] * (N_Z + 3),
        out_specs=HBM,
        out_shape=jax.ShapeDtypeStruct((SLOTS, PTS, LANES), BF),
        scratch_shapes=[
            pltpu.VMEM((SLOTS, RANK, LANES), BF),
            pltpu.VMEM((SLOTS, PTS, LANES), BF),
            pltpu.SemaphoreType.DMA((SLOTS,)),
        ],
        cost_estimate=pl.CostEstimate(flops=800_000_000, bytes_accessed=7_000_000, transcendentals=0),
        compiler_params=pltpu.CompilerParams(vmem_limit_bytes=14 << 20),
        name="tail",
    )(where, *local, *msgs, t_tail, synthesis)


def pipeline(features, analysis, transitions, synthesis):
    col = lax.axis_index("col")
    where = jnp.stack([lax.axis_index("row"), col >> 1, col & 1]).astype(jnp.int32)
    blocks = front(features, analysis, transitions)
    t_mid, t_tail = transitions[4:8], transitions[8:12]
    partner = lax.ppermute(blocks, "col", [(c, c ^ 1) for c in range(N_COL)])
    groups = []
    for b in range(2):
        group = list(messages(b, where, blocks, partner, t_mid))
        for d in FAR_FIRST + (0,):
            if b:
                group[d] = to_target_row(group[d], b, d)
            elif d:
                group[d] = z_swap(group[d], d)
        groups.append(group)
    merged = []
    for b in range(2):
        blocks = host_merge(groups[b])
        if b == 0:
            blocks = to_target_row(blocks, 0)
        merged.append(blocks)
    arrived = {}
    for d in FAR_FIRST:
        arrived[d] = z_swap(jnp.stack([merged[0][d], merged[1][d]]), d)
    return tail(where, merged, [arrived[d] for d in range(1, N_Z)], t_tail, synthesis)


def solution(mesh):
    in_specs = (
        P(("row", "col"), None, None),
        P(("row", "col"), None, None),
        P(None, ("row", "col"), None, None),
        P(("row", "col"), None, None),
    )
    out_specs = P(("row", "col"), None, None)
    return jax.shard_map(pipeline, mesh=mesh, in_specs=in_specs, out_specs=out_specs, check_vma=False)
```

```python
import functools

import jax
import jax.numpy as jnp
from jax import lax
from jax.experimental import pallas as pl
from jax.experimental.pallas import tpu as pltpu
from jax.sharding import PartitionSpec as P


RANK = 64
LANES = 512
PTS = 256
SLOTS = 16
N_ROW = 16
N_COL = 16
N_Z = 8
Z_LEVELS = 3
PAIR = 2 * RANK
MSG = LANES + Z_LEVELS * PAIR
BF = jnp.bfloat16
F32 = jnp.float32
VMEM = pl.BlockSpec(memory_space=pltpu.VMEM)
SMEM = pl.BlockSpec(memory_space=pltpu.SMEM)
HBM = pl.BlockSpec(memory_space=pltpu.HBM)
TOP = (8, 0)
TWIST = 6
FAR_FIRST = (4, 5, 3, 7, 6, 2, 1)


def base_of(r_ref):
    return r_ref[0] ^ r_ref[1] ^ (TWIST * r_ref[2])


def z_swap(array, d):
    return lax.ppermute(array, "col", [(c, c ^ (2 * d)) for c in range(N_COL)])


def to_target_row(array, b, d=0):
    pairs = []
    for r in range(N_ROW):
        for c in range(N_COL):
            to_col = c ^ (2 * d)
            to_row = r ^ (to_col >> 1) ^ TOP[b] ^ (TWIST * (c & 1))
            pairs.append((r * N_COL + c, to_row * N_COL + to_col))
    return lax.ppermute(array, ("row", "col"), pairs)


def dot(a, b):
    return lax.dot_general(a, b, (((1,), (0,)), ((), ())), preferred_element_type=F32)


def merge_pair(c_ref, lo, hi, t_lo, t_hi):
    joined = jnp.concatenate([c_ref[lo], c_ref[hi]], axis=0)
    merged = dot(jnp.concatenate([t_lo, t_hi], axis=0), joined).astype(BF)
    c_ref[lo] = merged[:RANK]
    c_ref[hi] = merged[RANK:]


def front_kernel(f_hbm, a_hbm, t_hbm, c_ref, f_buf, a_buf, t_buf, f_sem, t_sem, a_sem):
    f_copies = [pltpu.make_async_copy(f_hbm.at[l], f_buf.at[l], f_sem.at[l]) for l in range(SLOTS)]
    a_copies = [
        pltpu.make_async_copy(a_hbm.at[pl.ds(4 * i, 4)], a_buf.at[pl.ds(4 * i, 4)], a_sem.at[i]) for i in range(4)
    ]
    t_copies = [pltpu.make_async_copy(t_hbm.at[e], t_buf.at[e], t_sem.at[e]) for e in range(4)]
    for l in range(SLOTS):
        if l % 4 == 0:
            a_copies[l // 4].start()
        f_copies[l].start()
        if l in (3, 7):
            t_copies[2 * (l // 4)].start()
            t_copies[2 * (l // 4) + 1].start()

    def level(e, first, count):
        stride = 1 << e
        for lo in range(first, first + count):
            if not lo & stride:
                merge_pair(c_ref, lo, lo + stride, t_buf[e, lo], t_buf[e, lo + stride])

    for group in range(4):
        a_copies[group].wait()
        for l in range(4 * group, 4 * group + 4):
            f_copies[l].wait()
        if group == 1:
            t_copies[0].wait()
            t_copies[1].wait()
        if group == 3:
            t_copies[2].wait()
            t_copies[3].wait()
        for l in range(4 * group, 4 * group + 4):
            c_ref[l] = dot(a_buf[l], f_buf[l]).astype(BF)
        if group:
            level(0, 4 * group - 4, 4)
            level(1, 4 * group - 4, 4)
        if group == 3:
            level(2, 0, 8)
    level(0, 12, 4)
    level(1, 12, 4)
    level(2, 8, 8)
    level(3, 0, 16)


def front(features, analysis, transitions):
    return pl.pallas_call(
        front_kernel,
        in_specs=[HBM] * 3,
        out_specs=VMEM,
        out_shape=jax.ShapeDtypeStruct((SLOTS, RANK, LANES), BF),
        scratch_shapes=[
            pltpu.VMEM((SLOTS, PTS, LANES), BF),
            pltpu.VMEM((SLOTS, RANK, PTS), BF),
            pltpu.VMEM((4, SLOTS, RANK, PAIR), BF),
            pltpu.SemaphoreType.DMA((SLOTS,)),
            pltpu.SemaphoreType.DMA((4,)),
            pltpu.SemaphoreType.DMA((4,)),
        ],
        cost_estimate=pl.CostEstimate(flops=800_000_000, bytes_accessed=7_000_000, transcendentals=0),
        compiler_params=pltpu.CompilerParams(vmem_limit_bytes=65_600_000),
        name="front",
    )(features, analysis, transitions)


def message_kernel(b, r_ref, own_ref, partner_ref, t_ref, *outs):
    base, z = base_of(r_ref), r_ref[1]
    for core in range(2):

        @pl.when(r_ref[2] == core)
        def _(low=partner_ref if core else own_ref, high=own_ref if core else partner_ref):
            for d in range(N_Z):
                s = base ^ (d | TOP[b])
                joined = jnp.concatenate([low[s], high[s]], axis=0)
                outs[d][:, :LANES] = dot(t_ref[0, s], joined).astype(BF)
                for e in range(Z_LEVELS):
                    t = t_ref[1 + e, s]
                    flipped = jnp.concatenate([t[:, RANK:], t[:, :RANK]], axis=1)
                    host_bit = ((z ^ d) >> e) & 1
                    outs[d][:, LANES + e * PAIR : LANES + (e + 1) * PAIR] = jnp.where(host_bit == 0, t, flipped)


def messages(b, where, own, partner, t_mid):
    return pl.pallas_call(
        functools.partial(message_kernel, b),
        in_specs=[SMEM, VMEM, VMEM, VMEM],
        out_specs=[VMEM] * N_Z,
        out_shape=[jax.ShapeDtypeStruct((RANK, MSG), BF)] * N_Z,
        cost_estimate=pl.CostEstimate(flops=70_000_000, bytes_accessed=3_000_000, transcendentals=0),
        compiler_params=pltpu.CompilerParams(vmem_limit_bytes=8 << 20),
    )(where, own, partner, t_mid)


def host_kernel(*refs):
    msgs, out = refs[:N_Z], refs[N_Z]
    for e in range(Z_LEVELS):
        stride = 1 << e
        lanes = slice(LANES + e * PAIR, LANES + (e + 1) * PAIR)
        for lo in range(N_Z):
            if lo & stride:
                continue
            hi = lo + stride
            joined = [out[d] if e else msgs[d][:, :LANES] for d in (lo, hi)]
            weights = [msgs[d][:, lanes] for d in (lo, hi)]
            merged = dot(jnp.concatenate(weights, axis=0), jnp.concatenate(joined, axis=0)).astype(BF)
            out[lo] = merged[:RANK]
            out[hi] = merged[RANK:]


def host_merge(msgs):
    return pl.pallas_call(
        host_kernel,
        in_specs=[VMEM] * N_Z,
        out_specs=VMEM,
        out_shape=jax.ShapeDtypeStruct((N_Z, RANK, LANES), BF),
        cost_estimate=pl.CostEstimate(flops=200_000_000, bytes_accessed=1_400_000, transcendentals=0),
        compiler_params=pltpu.CompilerParams(vmem_limit_bytes=6 << 20),
    )(*msgs)


def tail_kernel(r_ref, *refs):
    local, msgs, (t_ref, s_ref, o_hbm, c_ref, o_buf, sem) = refs[:2], refs[2 : 1 + N_Z], refs[1 + N_Z :]
    base = base_of(r_ref)
    for b in range(2):
        c_ref[base ^ TOP[b]] = local[b][0]
        for d in range(1, N_Z):
            c_ref[base ^ (d | TOP[b])] = msgs[d - 1][b]
    for e in range(3):
        for lo in range(SLOTS):
            if not (lo >> e) & 1:
                hi = lo + (1 << e)
                merge_pair(c_ref, lo, hi, t_ref[e, lo], t_ref[e, hi])
    copies = []
    merge_pair(c_ref, 0, 8, t_ref[3, 0], t_ref[3, 8])
    merge_pair(c_ref, 1, 9, t_ref[3, 1], t_ref[3, 9])
    for j in range(N_Z):
        if j + 2 < N_Z:
            merge_pair(c_ref, j + 2, j + 10, t_ref[3, j + 2], t_ref[3, j + 10])
        for l in (j, j + 8):
            o_buf[l] = lax.dot_general(
                s_ref[l], c_ref[l], (((0,), (0,)), ((), ())), preferred_element_type=F32
            ).astype(BF)
            copies.append(pltpu.make_async_copy(o_buf.at[l], o_hbm.at[l], sem.at[l]))
            copies[-1].start()
    for copy in copies:
        copy.wait()


def tail(where, local, msgs, t_tail, synthesis):
    return pl.pallas_call(
        tail_kernel,
        in_specs=[SMEM] + [VMEM] * (N_Z + 3),
        out_specs=HBM,
        out_shape=jax.ShapeDtypeStruct((SLOTS, PTS, LANES), BF),
        scratch_shapes=[
            pltpu.VMEM((SLOTS, RANK, LANES), BF),
            pltpu.VMEM((SLOTS, PTS, LANES), BF),
            pltpu.SemaphoreType.DMA((SLOTS,)),
        ],
        cost_estimate=pl.CostEstimate(flops=800_000_000, bytes_accessed=7_000_000, transcendentals=0),
        compiler_params=pltpu.CompilerParams(vmem_limit_bytes=14 << 20),
        name="tail",
    )(where, *local, *msgs, t_tail, synthesis)


def pipeline(features, analysis, transitions, synthesis):
    col = lax.axis_index("col")
    where = jnp.stack([lax.axis_index("row"), col >> 1, col & 1]).astype(jnp.int32)
    blocks = front(features, analysis, transitions)
    t_mid, t_tail = transitions[4:8], transitions[8:12]
    partner = lax.ppermute(blocks, "col", [(c, c ^ 1) for c in range(N_COL)])
    groups = []
    for b in range(2):
        group = list(messages(b, where, blocks, partner, t_mid))
        for d in FAR_FIRST + (0,):
            if b:
                group[d] = to_target_row(group[d], b, d)
            elif d:
                group[d] = z_swap(group[d], d)
        groups.append(group)
    merged = []
    for b in range(2):
        blocks = host_merge(groups[b])
        if b == 0:
            blocks = to_target_row(blocks, 0)
        merged.append(blocks)
    arrived = {}
    for d in FAR_FIRST:
        arrived[d] = z_swap(jnp.stack([merged[0][d], merged[1][d]]), d)
    return tail(where, merged, [arrived[d] for d in range(1, N_Z)], t_tail, synthesis)


def solution(mesh):
    in_specs = (
        P(("row", "col"), None, None),
        P(("row", "col"), None, None),
        P(None, ("row", "col"), None, None),
        P(("row", "col"), None, None),
    )
    out_specs = P(("row", "col"), None, None)
    return jax.shard_map(pipeline, mesh=mesh, in_specs=in_specs, out_specs=out_specs, check_vma=False)
```
